256 devices in a mesh: kr: 32 (over z_lo, x, y), kc: 8 (over z_hi, core).
Axes of the slice: x: 4, y: 4, z: 8 (z_hi: 4, z_lo: 2; z = z_hi * 2 + z_lo), core: 2. Of those that a mesh axis runs over, the one named last changes fastest.
Arguments:
- pair_conduction: bfloat16 [768, 64, 4096], P('kr', None, 'kc'), may hold values from -6 to 6
- pair_valence: bfloat16 [768, 64, 4096], P('kr', None, 'kc'), may hold values from -6 to 6
- screened: bfloat16 [32, 4096, 4096], P('kr', 'kc'), may hold values from -0.09375 to 0.09375
- sphere_sizes: int32 [32], replicated, may hold values from 2048 to 4096, as said below
Outputs:
- kernels: float32 [768, 64, 64], P('kr', 'kc')
The draws below stay inside these ranges and needn't reach their ends.
Inputs may be any that keep to these rules, and one draw needn't show every extreme that they name: `sphere_sizes`: each q point's sphere holds 2048 to 4096 G-vectors, and some q point holds all 4096.
All inputs are finite; a program needn't handle non-finite values.
Results may differ from the reference program's by a relative error of at most 0.0029.
Values may be sent and summed in bfloat16 or wider, within the bound.
No kernel may reach another device: no remote copies, remote signals or barrier semaphores. Data moves between devices by JAX's collectives and lax.ppermute only.
A program may use at most 128 MiB of HBM per device.

```python
import jax
import jax.numpy as jnp
from jax import lax

G = 4096
NV = 8
NC = 8
PG = 8
NQ = 32
NP = 768


def draw_sphere_sizes(key, part):
    first_key, second_key = jax.random.split(jax.random.fold_in(key, 17))
    sampled = jax.random.randint(first_key, (NQ,), G // 2, G + 1)
    chosen = jax.random.randint(second_key, (), 0, NQ)
    return jnp.where(jnp.arange(NQ) == chosen, G, sampled).astype(jnp.int32)


def shard_levels(key, shape, cuts, low, largest):
    def one(axis_at, parts):
        draws = jax.random.uniform(jax.random.fold_in(jax.random.fold_in(key, 6), axis_at), (parts,), jnp.float32, low / len(cuts), largest / len(cuts))
        return jnp.repeat(jnp.exp(draws), shape[axis_at] // parts).reshape((-1,) + (1,) * (len(shape) - axis_at - 1))

    loudness = one(*cuts[0])
    for cut in cuts[1:]:
        loudness = loudness * one(*cut)
    return loudness


def gaussian(rng, dims, deviation, limit, cuts=(), kind=jnp.bfloat16):
    result = deviation * jax.random.normal(rng, dims, jnp.float32)
    if cuts:
        result = result * shard_levels(rng, dims, cuts, -0.22, 0.18)
    return jnp.clip(result, -limit, limit).astype(kind)


def setup_inputs(seed: int = 0) -> dict:
    splits = jax.random.split(jax.random.key(seed), 5)
    return {
        "pair_conduction": gaussian(splits[0], (NP, NC * NC, G), 1.0, 6.0, ((0, 32), (2, 8))),
        "pair_valence": gaussian(splits[1], (NP, NV * NV, G), 1.0, 6.0, ((0, 32), (2, 8))),
        "screened": gaussian(splits[2], (NQ, G, G), G ** -0.5, 0.09375, ((0, 32), (1, 8))),
        "sphere_sizes": draw_sphere_sizes(jax.random.fold_in(splits[4], 71), 0),
    }


prefactor = 0.015625


def restrict(screen_q, sphere):
    gvector_ids = jnp.arange(G, dtype=jnp.int32)
    inside = gvector_ids < sphere
    keep = inside[:, None] & inside[None, :]
    return jnp.where(keep, screen_q, jnp.zeros((), screen_q.dtype))


def reference(pair_conduction, pair_valence, screened, sphere_sizes):
    conduction = pair_conduction.reshape(NQ, 3, PG, NC * NC, G)
    valence = pair_valence.reshape(NQ, 3, PG, NV * NV, G)

    def one_owner(owner_index):
        results = []
        for group_index, offset in ((0, 0), (1, -1), (2, 1)):
            q_index = (owner_index + offset) % NQ
            screen_q = restrict(screened[q_index], sphere_sizes[q_index])
            applied = jnp.einsum('pbh,gh->pbg', valence[owner_index, group_index].astype(jnp.float32),
                                 screen_q.astype(jnp.float32)).astype(jnp.bfloat16)
            kern_block = jnp.einsum('pag,pbg->pab', conduction[owner_index, group_index].astype(jnp.float32),
                                    applied.astype(jnp.float32))
            results.append(kern_block * prefactor)
        return jnp.stack(results)

    stacked = lax.map(one_owner, jnp.arange(NQ, dtype=jnp.int32))
    return stacked.reshape(NP, NC * NC, NV * NV)
```

```python
import jax
import jax.numpy as jnp
from jax import lax
from jax.sharding import PartitionSpec as P

prefactor = 0.015625
AXES = ("kr", "kc")


def moves(owners, quarters, target):
    pairs = []
    for i in range(owners):
        for k in range(quarters):
            for c in range(2):
                ti, tk, tc = target(i, k, c)
                pairs.append(
                    (
                        (i * quarters + k) * 2 + c,
                        ((ti % owners) * quarters + tk % quarters) * 2 + tc,
                    )
                )
    return pairs


def turn(group, q, owners):
    if group == 1:
        return -1 if q == owners - 1 else 1
    if group == 2:
        return 1 if q == 0 else -1
    return 1


def shards(pair_conduction, pair_valence, screened, sphere_sizes):
    owners = lax.axis_size("kr")
    quarters = lax.axis_size("kc") // 2
    rows = screened.shape[1]
    group_size = pair_valence.shape[0] // 3
    bands = pair_valence.shape[1]
    cbands = pair_conduction.shape[1]
    half = group_size // 2
    owner = lax.axis_index("kr")
    place = lax.axis_index("kc")
    quarter = place // 2
    core = place % 2
    slab = screened[0]
    sphere = sphere_sizes[owner]

    def send(x, target):
        return lax.ppermute(x, AXES, moves(owners, quarters, target))

    swap = lambda x: send(x, lambda i, k, c: (i, k, 1 - c))
    shift = (0, -1, 1)
    v = [pair_valence[g * group_size : (g + 1) * group_size] for g in range(3)]
    cond = [pair_conduction[g * group_size : (g + 1) * group_size] for g in range(3)]

    own, ahead, behind, far = {}, {}, {}, {}
    for g in (1, 2):
        own[g] = send(v[g], lambda i, k, c: (i + shift[g], k, c))
    own[0] = v[0]
    for g in (1, 2, 0):
        ahead[g] = send(
            v[g],
            lambda i, k, c: (
                i + shift[g],
                k + turn(g, (i + shift[g]) % owners, owners),
                c,
            ),
        )
    for g in (1, 2, 0):
        behind[g] = send(own[g], lambda i, k, c: (i, k - turn(g, i, owners), c))
    for g in (1, 2, 0):
        far[g] = (
            send(ahead[g][:half], lambda i, k, c: (i, k + turn(g, i, owners), c)),
            send(behind[g][half:], lambda i, k, c: (i, k - turn(g, i, owners), c)),
        )

    def columns(which):
        first_row = place * rows
        parts = [
            lax.dynamic_slice_in_dim(slab, (2 * j + which) * rows, rows, 1)
            for j in range(quarters)
        ]
        row_inside = first_row + jnp.arange(rows, dtype=jnp.int32) < sphere
        col = jnp.arange(rows, dtype=jnp.int32)
        zero = jnp.zeros((), slab.dtype)
        return jnp.concatenate(
            [
                jnp.where(
                    row_inside[:, None] & ((2 * j + which) * rows + col < sphere)[None],
                    parts[j],
                    zero,
                )
                for j in range(quarters)
            ],
            1,
        )

    w = jnp.concatenate([columns(core), swap(columns(1 - core))], 0)

    cfull = {}
    for g in range(3):
        mine = (
            cond[g] if g == 0 else send(cond[g], lambda i, k, c: (i + shift[g], k, c))
        )
        cfull[g] = jnp.concatenate([mine, swap(mine)], 2)

    def wblock(j):
        return lax.dynamic_slice_in_dim(w, (j % quarters) * rows, rows, 1)

    def mul(x, j):
        return lax.dot_general(
            x, wblock(j), (((2,), (1,)), ((), ())), preferred_element_type=jnp.float32
        )

    results = [None] * 3
    for g in (1, 2, 0):
        sigma = 1
        if g == 1:
            sigma = jnp.where(owner == owners - 1, -1, 1)
        if g == 2:
            sigma = jnp.where(owner == 0, 1, -1)
        total = mul(own[g], quarter)
        total += mul(ahead[g], quarter - sigma + quarters)
        total += mul(behind[g], quarter + sigma + quarters)
        total += mul(jnp.concatenate(far[g], 0), quarter + 2)
        high = lax.reduce_precision(total, 8, 7)
        low = (total - high).astype(jnp.bfloat16)
        high = high.astype(jnp.bfloat16)

        def pairwise(applied):
            return jnp.einsum(
                "pag,pbg->pab", cfull[g], applied, preferred_element_type=jnp.float32
            )

        part = pairwise(high) + pairwise(low)
        part = part.reshape(group_size, quarters, 2, cbands // quarters // 2, bands)
        keep = lax.dynamic_index_in_dim(part, core, 2, False)
        give = lax.dynamic_index_in_dim(part, 1 - core, 2, False)
        keep = keep + swap(give)
        out = None
        for d in range(quarters):
            block = lax.dynamic_index_in_dim(keep, (quarter + d) % quarters, 1, False)
            if d or g:
                block = send(block, lambda i, k, c: (i - shift[g], k + d, c))
            out = block if out is None else out + block
        results[g] = out * prefactor
    return jnp.concatenate(results, 0)


def solution(mesh):
    return jax.shard_map(
        shards,
        mesh=mesh,
        in_specs=(P("kr", None, "kc"), P("kr", None, "kc"), P("kr", "kc", None), P()),
        out_specs=P("kr", "kc", None),
        check_vma=False,
    )
```

```python
import functools

import jax
import jax.numpy as jnp
from jax import lax
from jax.experimental import pallas as pl
from jax.experimental.pallas import tpu as pltpu
from jax.sharding import PartitionSpec as P

prefactor = 0.015625
AXES = ("kr", "kc")
VMEM = pl.BlockSpec(memory_space=pltpu.VMEM)
SMEM = pl.BlockSpec(memory_space=pltpu.SMEM)
CONTRACT_LAST = (((1,), (1,)), ((), ()))


def moves(owners, quarters, target):
    pairs = []
    for i in range(owners):
        for k in range(quarters):
            for c in range(2):
                ti, tk, tc = target(i, k, c)
                pairs.append(
                    (
                        (i * quarters + k) * 2 + c,
                        ((ti % owners) * quarters + tk % quarters) * 2 + tc,
                    )
                )
    return pairs


def turn(group, q, owners):
    if group == 1:
        return -1 if q == owners - 1 else 1
    if group == 2:
        return 1 if q == 0 else -1
    return 1


def restrict_kernel(quarters, rows, info_ref, slab_ref, mine_ref, give_ref):
    core, sphere = info_ref[0], info_ref[2]
    block = slab_ref.shape[0]
    first = info_ref[1] + pl.program_id(0) * block
    row = first + lax.broadcasted_iota(jnp.int32, (block, rows), 0)
    col = lax.broadcasted_iota(jnp.int32, (block, rows), 1)
    row_inside = row < sphere
    for j in range(quarters):
        kept = []
        for t in range(2):
            at = (2 * j + t) * rows
            keep = row_inside & (at + col < sphere)
            x = slab_ref[:, at : at + rows].astype(jnp.float32)
            kept.append(jnp.where(keep, x, 0.0))
        even = core == 0
        span = pl.ds(j * rows, rows)
        mine_ref[:, span] = jnp.where(even, kept[0], kept[1]).astype(mine_ref.dtype)
        give_ref[:, span] = jnp.where(even, kept[1], kept[0]).astype(give_ref.dtype)


def first_kernel(group_size, bands, rows, info_ref, own, ahead, behind, w0, w1, acc):
    for s, w in enumerate((w0, w1)):
        total = None
        for n, x in enumerate((own, ahead, behind)):
            at = pl.multiple_of(info_ref[n] * rows, rows)
            y = lax.dot_general(
                x[...].reshape(group_size * bands, rows),
                w[:, pl.ds(at, rows)],
                CONTRACT_LAST,
                preferred_element_type=jnp.float32,
            )
            total = y if total is None else total + y
        acc[s] = total


def last_kernel(
    sizes, info_ref, acc, far0, far1, w0, w1, c0, c1, keep_ref, give_ref
):
    group_size, bands, rows, quarters = sizes
    half = group_size // 2
    at = pl.multiple_of(info_ref[0] * rows, rows)
    quarter, core = info_ref[1], info_ref[2]
    for h, x in enumerate((far0, far1)):
        base = h * half * bands
        high, low = [], []
        for s, w in enumerate((w0, w1)):
            y = acc[s, base : base + half * bands] + lax.dot_general(
                x[...].reshape(half * bands, rows),
                w[:, pl.ds(at, rows)],
                CONTRACT_LAST,
                preferred_element_type=jnp.float32,
            )
            top = y.astype(jnp.bfloat16)
            high.append(top)
            low.append((y - top.astype(jnp.float32)).astype(jnp.bfloat16))
        for n in range(half):
            p = h * half + n
            part = None
            for s, c in enumerate((c0, c1)):
                for piece in (high[s], low[s]):
                    y = lax.dot_general(
                        c[p],
                        piece[n * bands : (n + 1) * bands],
                        CONTRACT_LAST,
                        preferred_element_type=jnp.float32,
                    )
                    part = y if part is None else part + y
            part = part * prefactor
            part = part.reshape(quarters, 2, -1, part.shape[-1])
            even = core == 0
            for j in range(quarters):
                d = lax.rem(j - quarter + quarters, quarters)
                keep_ref[d, p] = jnp.where(even, part[j, 0], part[j, 1])
                give_ref[d, p] = jnp.where(even, part[j, 1], part[j, 0])


def shards(pair_conduction, pair_valence, screened, sphere_sizes):
    owners = lax.axis_size("kr")
    quarters = lax.axis_size("kc") // 2
    rows, gvectors = screened.shape[1:]
    group_size = pair_valence.shape[0] // 3
    bands = pair_valence.shape[1]
    cbands = pair_conduction.shape[1]
    half = group_size // 2
    owner = lax.axis_index("kr")
    place = lax.axis_index("kc")
    quarter = place // 2
    core = place % 2
    shift = (0, -1, 1)

    def send(x, target):
        return lax.ppermute(x, AXES, moves(owners, quarters, target))

    def swap(x):
        return send(x, lambda i, k, c: (i, k, 1 - c))

    v = [pair_valence[g * group_size : (g + 1) * group_size] for g in range(3)]
    cond = [pair_conduction[g * group_size : (g + 1) * group_size] for g in range(3)]
    sigma = (
        jnp.int32(1),
        jnp.where(owner == owners - 1, -1, 1),
        jnp.where(owner == 0, 1, -1),
    )

    own, ahead, behind = {0: v[0]}, {}, {}
    for g in (1, 2):
        own[g] = send(v[g], lambda i, k, c: (i + shift[g], k, c))
    for g in (1, 2):
        ahead[g] = send(
            v[g],
            lambda i, k, c: (
                i + shift[g],
                k + turn(g, (i + shift[g]) % owners, owners),
                c,
            ),
        )
    c_own = {0: cond[0]}
    for g in (1, 2):
        c_own[g] = send(cond[g], lambda i, k, c: (i + shift[g], k, c))
    for g in (1, 2):
        behind[g] = send(own[g], lambda i, k, c: (i, k - turn(g, i, owners), c))
    up = [
        send(v[0][h * half : (h + 1) * half], lambda i, k, c: (i, k + 1, c))
        for h in range(2)
    ]
    down = [
        send(v[0][h * half : (h + 1) * half], lambda i, k, c: (i, k - 1, c))
        for h in (1, 0)
    ][::-1]
    forward_up, forward_down = [], []
    for g in (1, 2):
        forward_up.append(
            jnp.where(sigma[g] > 0, ahead[g][:half], behind[g][:half])
        )
        forward_down.append(
            jnp.where(sigma[g] > 0, behind[g][half:], ahead[g][half:])
        )
    far_up = send(jnp.concatenate(forward_up, 0), lambda i, k, c: (i, k + 1, c))
    far_down = send(jnp.concatenate(forward_down, 0), lambda i, k, c: (i, k - 1, c))
    far = {
        1: (far_up[:half], far_down[:half]),
        2: (far_up[half:], far_down[half:]),
        0: (
            send(up[0], lambda i, k, c: (i, k + 1, c)),
            send(down[1], lambda i, k, c: (i, k - 1, c)),
        ),
    }
    ahead[0] = jnp.concatenate(up, 0)
    behind[0] = jnp.concatenate(down, 0)

    info = jnp.stack([core, place * rows, sphere_sizes[owner]])
    block = rows // 4
    w0, give = pl.pallas_call(
        functools.partial(restrict_kernel, quarters, rows),
        grid=(rows // block,),
        in_specs=[SMEM, pl.BlockSpec((block, gvectors), lambda r: (r, 0))],
        out_specs=[pl.BlockSpec((block, gvectors // 2), lambda r: (r, 0))] * 2,
        out_shape=[jax.ShapeDtypeStruct((rows, gvectors // 2), screened.dtype)] * 2,
        name="restrict",
    )(info, screened[0])
    w1 = swap(give)
    c_par = {g: swap(c_own[g]) for g in range(3)}

    kept, given = {}, {}
    for g in (1, 2, 0):
        at = jnp.stack(
            [
                quarter,
                lax.rem(quarter - sigma[g] + quarters, quarters),
                lax.rem(quarter + sigma[g] + quarters, quarters),
            ]
        )
        acc = pl.pallas_call(
            functools.partial(first_kernel, group_size, bands, rows),
            in_specs=[SMEM] + [VMEM] * 5,
            out_specs=VMEM,
            out_shape=jax.ShapeDtypeStruct((2, group_size * bands, rows), jnp.float32),
        )(at, own[g], ahead[g], behind[g], w0, w1)
        at = jnp.stack([lax.rem(quarter + 2, quarters), quarter, core])
        shape = (quarters, group_size, cbands // quarters // 2, bands)
        kept[g], given[g] = pl.pallas_call(
            functools.partial(last_kernel, (group_size, bands, rows, quarters)),
            in_specs=[SMEM] + [VMEM] * 7,
            out_specs=[VMEM] * 2,
            out_shape=[jax.ShapeDtypeStruct(shape, jnp.float32)] * 2,
        )(at, acc, *far[g], w0, w1, c_own[g], c_par[g])

    def exchange(keep, give):
        keep = keep + swap(give)
        out = keep[0]
        for d in (1, 3, 2):
            out = out + send(keep[d], lambda i, k, c: (i, k + d, c))
        return out

    both = exchange(
        jnp.concatenate([kept[1], kept[2]], 1), jnp.concatenate([given[1], given[2]], 1)
    )
    results = [
        send(
            both[(g - 1) * group_size : g * group_size],
            lambda i, k, c: (i - shift[g], k, c),
        )
        for g in (1, 2)
    ]
    results.insert(0, exchange(kept[0], given[0]))
    return jnp.concatenate(results, 0)


def solution(mesh):
    return jax.shard_map(
        shards,
        mesh=mesh,
        in_specs=(P("kr", None, "kc"), P("kr", None, "kc"), P("kr", "kc", None), P()),
        out_specs=P("kr", "kc", None),
        check_vma=False,
    )
```

```python
import functools

import jax
import jax.numpy as jnp
from jax import lax
from jax.experimental import pallas as pl
from jax.experimental.pallas import tpu as pltpu
from jax.sharding import PartitionSpec as P


prefactor = 0.015625
AXES = ("kr", "kc")
VMEM = pl.BlockSpec(memory_space=pltpu.VMEM)
SMEM = pl.BlockSpec(memory_space=pltpu.SMEM)
CONTRACT_LAST = (((1,), (1,)), ((), ()))


def moves(owners, quarters, target):
    pairs = []
    for i in range(owners):
        for k in range(quarters):
            for c in range(2):
                ti, tk, tc = target(i, k, c)
                pairs.append(
                    (
                        (i * quarters + k) * 2 + c,
                        ((ti % owners) * quarters + tk % quarters) * 2 + tc,
                    )
                )
    return pairs


def turn(group, q, owners):
    if group == 1:
        return -1 if q == owners - 1 else 1
    if group == 2:
        return 1 if q == 0 else -1
    return 1


def where_am_i():
    place = lax.axis_index("kc")
    return lax.axis_index("kr"), lax.div(place, 2), lax.rem(place, 2)


def heading(group, owner, owners):
    if group == 1:
        return jnp.where(owner == owners - 1, -1, 1)
    if group == 2:
        return jnp.where(owner == 0, 1, -1)
    return jnp.int32(1)


def restrict_kernel(quarters, rows, spheres_ref, slab_ref, mine_ref, give_ref):
    owner, quarter, core = where_am_i()
    sphere = spheres_ref[owner]
    block = slab_ref.shape[0]
    first = (2 * quarter + core) * rows + pl.program_id(0) * block
    row = first + lax.broadcasted_iota(jnp.int32, (block, rows), 0)
    col = lax.broadcasted_iota(jnp.int32, (block, rows), 1)
    row_inside = row < sphere
    even = core == 0
    for j in range(quarters):
        kept = []
        for t in range(2):
            at = (2 * j + t) * rows
            keep = row_inside & (at + col < sphere)
            x = slab_ref[:, at : at + rows].astype(jnp.float32)
            kept.append(jnp.where(keep, x, 0.0))
        span = pl.ds(j * rows, rows)
        mine_ref[:, span] = jnp.where(even, kept[0], kept[1]).astype(mine_ref.dtype)
        give_ref[:, span] = jnp.where(even, kept[1], kept[0]).astype(give_ref.dtype)


def forward_kernel(owners, half, a1, b1, a2, b2, up_ref, down_ref):
    owner, _, _ = where_am_i()
    for n, (a, b) in enumerate(((a1, b1), (a2, b2))):
        ahead_up = heading(n + 1, owner, owners) > 0

        @pl.when(ahead_up)
        def _():
            up_ref[n * half : (n + 1) * half] = a[:half]
            down_ref[n * half : (n + 1) * half] = b[half:]

        @pl.when(jnp.logical_not(ahead_up))
        def _():
            up_ref[n * half : (n + 1) * half] = b[:half]
            down_ref[n * half : (n + 1) * half] = a[half:]


def flat(x):
    x = x[...]
    return x.reshape(x.shape[0] * x.shape[1], x.shape[2])


def first_kernel(group, owners, quarters, counts, *refs):
    blocks, (w0, w1, acc) = refs[:-3], refs[-3:]
    owner, quarter, _ = where_am_i()
    rows = acc.shape[2]
    sigma = heading(group, owner, owners)
    columns = (
        quarter,
        lax.rem(quarter - sigma + quarters, quarters),
        lax.rem(quarter + sigma + quarters, quarters),
    )
    for s, w in enumerate((w0, w1)):
        base, size = 0, acc.shape[1]
        for h in range(counts):
            total = None
            for n in range(3):
                pieces = blocks[n * counts : (n + 1) * counts]
                at = pl.multiple_of(columns[n] * rows, rows)
                y = lax.dot_general(
                    flat(pieces[h]),
                    w[:, pl.ds(at, rows)],
                    CONTRACT_LAST,
                    preferred_element_type=jnp.float32,
                )
                total = y if total is None else total + y
            acc[s, base : base + size // counts] = total
            base += size // counts


def last_kernel(groups, quarters, half, *refs):
    accs, refs = refs[:groups], refs[groups:]
    far, (w0, w1), refs = refs[:2], refs[2:4], refs[4:]
    conduction, (keep_ref, give_ref) = refs[:-2], refs[-2:]
    _, quarter, core = where_am_i()
    bands, rows = far[0].shape[1:]
    at = pl.multiple_of(lax.rem(quarter + 2, quarters) * rows, rows)
    even = core == 0
    for g in range(groups):
        for h, x in enumerate(far):
            base = h * half * bands
            both = []
            for s, w in enumerate((w0, w1)):
                y = accs[g][s, base : base + half * bands] + lax.dot_general(
                    x[g * half : (g + 1) * half].reshape(half * bands, rows),
                    w[:, pl.ds(at, rows)],
                    CONTRACT_LAST,
                    preferred_element_type=jnp.float32,
                )
                high = y.astype(jnp.bfloat16)
                low = (y - high.astype(jnp.float32)).astype(jnp.bfloat16)
                both.append((high, low))
            for n in range(half):
                p = h * half + n
                part = None
                for s in range(2):
                    c = conduction[2 * g + s]
                    span = slice(n * bands, (n + 1) * bands)
                    y = lax.dot_general(
                        c[p],
                        jnp.concatenate([both[s][0][span], both[s][1][span]], 0),
                        CONTRACT_LAST,
                        preferred_element_type=jnp.float32,
                    )
                    part = y if part is None else part + y
                part = (part[:, :bands] + part[:, bands:]) * prefactor
                part = part.reshape(quarters, 2, -1, bands)
                for j in range(quarters):
                    d = lax.rem(j - quarter + quarters, quarters)
                    q = g * 2 * half + p
                    keep_ref[d, q] = jnp.where(even, part[j, 0], part[j, 1])
                    give_ref[d, q] = jnp.where(even, part[j, 1], part[j, 0])


def shards(pair_conduction, pair_valence, screened, sphere_sizes):
    owners = lax.axis_size("kr")
    quarters = lax.axis_size("kc") // 2
    rows, gvectors = screened.shape[1:]
    group_size = pair_valence.shape[0] // 3
    bands = pair_valence.shape[1]
    cbands = pair_conduction.shape[1]
    half = group_size // 2
    shift = (0, -1, 1)
    params = pltpu.CompilerParams(vmem_limit_bytes=24 * 2**20)

    def send(x, target):
        return lax.ppermute(x, AXES, moves(owners, quarters, target))

    def swap(x):
        return send(x, lambda i, k, c: (i, k, 1 - c))

    def call(body, out_shape, operands, in_specs=None, out_specs=None, **kw):
        many = isinstance(out_shape, list)
        return pl.pallas_call(
            body,
            in_specs=in_specs or [VMEM] * len(operands),
            out_specs=out_specs or ([VMEM] * len(out_shape) if many else VMEM),
            out_shape=out_shape,
            compiler_params=params,
            **kw,
        )(*operands)

    v = [pair_valence[g * group_size : (g + 1) * group_size] for g in range(3)]
    cond = [pair_conduction[g * group_size : (g + 1) * group_size] for g in range(3)]

    own, ahead, behind = {}, {}, {}
    for g in (1, 2):
        own[g] = send(v[g], lambda i, k, c: (i + shift[g], k, c))
    for g in (1, 2):
        ahead[g] = send(
            v[g],
            lambda i, k, c: (
                i + shift[g],
                k + turn(g, (i + shift[g]) % owners, owners),
                c,
            ),
        )
    c_own = {0: cond[0]}
    for g in (1, 2):
        c_own[g] = send(cond[g], lambda i, k, c: (i + shift[g], k, c))
    for g in (1, 2):
        behind[g] = send(own[g], lambda i, k, c: (i, k - turn(g, i, owners), c))
    v0 = [v[0][:half], v[0][half:]]
    up, down = [None, None], [None, None]
    for n in range(2):
        up[n] = send(v0[n], lambda i, k, c: (i, k + 1, c))
        down[1 - n] = send(v0[1 - n], lambda i, k, c: (i, k - 1, c))
    going_up, going_down = call(
        functools.partial(forward_kernel, owners, half),
        [jax.ShapeDtypeStruct(v[0].shape, v[0].dtype)] * 2,
        (ahead[1], behind[1], ahead[2], behind[2]),
    )
    far = (
        send(going_up, lambda i, k, c: (i, k + 1, c)),
        send(going_down, lambda i, k, c: (i, k - 1, c)),
    )
    far0 = (
        send(up[0], lambda i, k, c: (i, k + 1, c)),
        send(down[1], lambda i, k, c: (i, k - 1, c)),
    )

    block = rows // 4
    w0, give = call(
        functools.partial(restrict_kernel, quarters, rows),
        [jax.ShapeDtypeStruct((rows, gvectors // 2), screened.dtype)] * 2,
        (sphere_sizes, screened[0]),
        in_specs=[SMEM, pl.BlockSpec((block, gvectors), lambda r: (r, 0))],
        out_specs=[pl.BlockSpec((block, gvectors // 2), lambda r: (r, 0))] * 2,
        grid=(rows // block,),
    )
    w1 = swap(give)
    c_par = {g: swap(c_own[g]) for g in range(3)}

    def first(g, counts, blocks):
        return call(
            functools.partial(first_kernel, g, owners, quarters, counts),
            jax.ShapeDtypeStruct((2, group_size * bands, rows), jnp.float32),
            (*blocks, w0, w1),
        )

    def last(groups, accs, far):
        shape = (
            quarters,
            len(groups) * group_size,
            cbands // quarters // 2,
            bands,
        )
        conduction = [x[g] for g in groups for x in (c_own, c_par)]
        return call(
            functools.partial(last_kernel, len(groups), quarters, half),
            [jax.ShapeDtypeStruct(shape, jnp.float32)] * 2,
            (*accs, *far, w0, w1, *conduction),
        )

    def exchange(keep, give):
        keep = keep + swap(give)
        parts = [send(keep[d], lambda i, k, c: (i, k + d, c)) for d in (1, 3, 2)]
        return keep[0] + parts[0] + parts[1] + parts[2]

    accs = [first(g, 1, (own[g], ahead[g], behind[g])) for g in (1, 2)]
    both = exchange(*last((1, 2), accs, far))
    results = [
        send(
            both[(g - 1) * group_size : g * group_size],
            lambda i, k, c: (i - shift[g], k, c),
        )
        for g in (1, 2)
    ]
    acc = first(0, 2, (*v0, *up, *down))
    results.insert(0, exchange(*last((0,), [acc], far0)))
    return jnp.concatenate(results, 0)


def solution(mesh):
    return jax.shard_map(
        shards,
        mesh=mesh,
        in_specs=(P("kr", None, "kc"), P("kr", None, "kc"), P("kr", "kc", None), P()),
        out_specs=P("kr", "kc", None),
        check_vma=False,
    )
```

```python
import functools

import jax
import jax.numpy as jnp
from jax import lax
from jax.experimental import pallas as pl
from jax.experimental.pallas import tpu as pltpu
from jax.sharding import PartitionSpec as P


prefactor = 0.015625
AXES = ("kr", "kc")
VMEM = pl.BlockSpec(memory_space=pltpu.VMEM)
SMEM = pl.BlockSpec(memory_space=pltpu.SMEM)
CONTRACT_LAST = (((1,), (1,)), ((), ()))


def moves(owners, quarters, target):
    pairs = []
    for i in range(owners):
        for k in range(quarters):
            for c in range(2):
                ti, tk, tc = target(i, k, c)
                pairs.append(
                    (
                        (i * quarters + k) * 2 + c,
                        ((ti % owners) * quarters + tk % quarters) * 2 + tc,
                    )
                )
    return pairs


def turn(group, q, owners):
    return 1 if group == 0 or q < owners // 2 else -1


def where_am_i():
    place = lax.axis_index("kc")
    return lax.axis_index("kr"), lax.div(place, 2), lax.rem(place, 2)


def heading(group, owner, owners):
    return jnp.int32(1) if group == 0 else jnp.where(owner < owners // 2, 1, -1)


def restrict_kernel(quarters, rows, spheres_ref, slab_ref, mine_ref, give_ref):
    owner, quarter, core = where_am_i()
    sphere = spheres_ref[owner]
    block = slab_ref.shape[0]
    first = (2 * quarter + core) * rows + pl.program_id(0) * block
    row = first + lax.broadcasted_iota(jnp.int32, (block, rows), 0)
    col = lax.broadcasted_iota(jnp.int32, (block, rows), 1)
    row_inside = row < sphere
    even = core == 0
    for j in range(quarters):
        kept = []
        for t in range(2):
            at = (2 * j + t) * rows
            keep = row_inside & (at + col < sphere)
            x = slab_ref[:, at : at + rows].astype(jnp.float32)
            kept.append(jnp.where(keep, x, 0.0))
        span = pl.ds(j * rows, rows)
        mine_ref[:, span] = jnp.where(even, kept[0], kept[1]).astype(mine_ref.dtype)
        give_ref[:, span] = jnp.where(even, kept[1], kept[0]).astype(give_ref.dtype)


def forward_kernel(owners, half, a1, b1, a2, b2, up_ref, down_ref):
    owner, _, _ = where_am_i()
    for n, (a, b) in enumerate(((a1, b1), (a2, b2))):
        ahead_up = heading(n + 1, owner, owners) > 0

        @pl.when(ahead_up)
        def _():
            up_ref[n * half : (n + 1) * half] = a[:half]
            down_ref[n * half : (n + 1) * half] = b[half:]

        @pl.when(jnp.logical_not(ahead_up))
        def _():
            up_ref[n * half : (n + 1) * half] = b[:half]
            down_ref[n * half : (n + 1) * half] = a[half:]


def flat(x):
    x = x[...]
    return x.reshape(x.shape[0] * x.shape[1], x.shape[2])


def first_kernel(group, owners, quarters, counts, *refs):
    blocks, (w0, w1, acc) = refs[:-3], refs[-3:]
    owner, quarter, _ = where_am_i()
    rows = acc.shape[2]
    sigma = heading(group, owner, owners)
    columns = (
        quarter,
        lax.rem(quarter - sigma + quarters, quarters),
        lax.rem(quarter + sigma + quarters, quarters),
    )
    for s, w in enumerate((w0, w1)):
        base, size = 0, acc.shape[1]
        for h in range(counts):
            total = None
            for n in range(3):
                pieces = blocks[n * counts : (n + 1) * counts]
                at = pl.multiple_of(columns[n] * rows, rows)
                y = lax.dot_general(
                    flat(pieces[h]),
                    w[:, pl.ds(at, rows)],
                    CONTRACT_LAST,
                    preferred_element_type=jnp.float32,
                )
                total = y if total is None else total + y
            acc[s, base : base + size // counts] = total
            base += size // counts


def last_kernel(groups, quarters, half, *refs):
    accs, refs = refs[:groups], refs[groups:]
    far, (w0, w1), refs = refs[:2], refs[2:4], refs[4:]
    conduction, (keep_ref, give_ref) = refs[:-2], refs[-2:]
    _, quarter, core = where_am_i()
    bands, rows = far[0].shape[1:]
    at = pl.multiple_of(lax.rem(quarter + 2, quarters) * rows, rows)
    even = core == 0
    for g in range(groups):
        for h, x in enumerate(far):
            base = h * half * bands
            both = []
            for s, w in enumerate((w0, w1)):
                y = accs[g][s, base : base + half * bands] + lax.dot_general(
                    x[g * half : (g + 1) * half].reshape(half * bands, rows),
                    w[:, pl.ds(at, rows)],
                    CONTRACT_LAST,
                    preferred_element_type=jnp.float32,
                )
                high = y.astype(jnp.bfloat16)
                low = (y - high.astype(jnp.float32)).astype(jnp.bfloat16)
                both.append((high, low))
            for n in range(half):
                p = h * half + n
                part = None
                for s in range(2):
                    c = conduction[2 * g + s]
                    span = slice(n * bands, (n + 1) * bands)
                    y = lax.dot_general(
                        c[p],
                        jnp.concatenate([both[s][0][span], both[s][1][span]], 0),
                        CONTRACT_LAST,
                        preferred_element_type=jnp.float32,
                    )
                    part = y if part is None else part + y
                part = (part[:, :bands] + part[:, bands:]) * prefactor
                part = part.reshape(quarters, 2, -1, bands)
                for j in range(quarters):
                    d = lax.rem(j - quarter + quarters, quarters)
                    q = g * 2 * half + p
                    keep_ref[d, q] = jnp.where(even, part[j, 0], part[j, 1])
                    give_ref[d, q] = jnp.where(even, part[j, 1], part[j, 0])


def shards(pair_conduction, pair_valence, screened, sphere_sizes):
    owners = lax.axis_size("kr")
    quarters = lax.axis_size("kc") // 2
    rows, gvectors = screened.shape[1:]
    group_size = pair_valence.shape[0] // 3
    bands = pair_valence.shape[1]
    cbands = pair_conduction.shape[1]
    half = group_size // 2
    shift = (0, -1, 1)
    params = pltpu.CompilerParams(vmem_limit_bytes=24 * 2**20)

    def send(x, target):
        return lax.ppermute(x, AXES, moves(owners, quarters, target))

    def swap(x):
        return send(x, lambda i, k, c: (i, k, 1 - c))

    def call(body, out_shape, operands, in_specs=None, out_specs=None, **kw):
        many = isinstance(out_shape, list)
        return pl.pallas_call(
            body,
            in_specs=in_specs or [VMEM] * len(operands),
            out_specs=out_specs or ([VMEM] * len(out_shape) if many else VMEM),
            out_shape=out_shape,
            compiler_params=params,
            **kw,
        )(*operands)

    v = [pair_valence[g * group_size : (g + 1) * group_size] for g in range(3)]
    cond = [pair_conduction[g * group_size : (g + 1) * group_size] for g in range(3)]

    own, ahead, behind = {}, {}, {}
    for g in (1, 2):
        own[g] = send(v[g], lambda i, k, c: (i + shift[g], k, c))
    for g in (1, 2):
        ahead[g] = send(
            v[g],
            lambda i, k, c: (
                i + shift[g],
                k + turn(g, (i + shift[g]) % owners, owners),
                c,
            ),
        )
    c_own = {0: cond[0]}
    for g in (1, 2):
        c_own[g] = send(cond[g], lambda i, k, c: (i + shift[g], k, c))
    for g in (1, 2):
        behind[g] = send(own[g], lambda i, k, c: (i, k - turn(g, i, owners), c))
    v0 = [v[0][:half], v[0][half:]]
    up, down = [None, None], [None, None]
    for n in range(2):
        up[n] = send(v0[n], lambda i, k, c: (i, k + 1, c))
        down[1 - n] = send(v0[1 - n], lambda i, k, c: (i, k - 1, c))
    going_up, going_down = call(
        functools.partial(forward_kernel, owners, half),
        [jax.ShapeDtypeStruct(v[0].shape, v[0].dtype)] * 2,
        (ahead[1], behind[1], ahead[2], behind[2]),
    )
    far = (
        send(going_up, lambda i, k, c: (i, k + 1, c)),
        send(going_down, lambda i, k, c: (i, k - 1, c)),
    )
    far0 = (
        send(up[0], lambda i, k, c: (i, k + 1, c)),
        send(down[1], lambda i, k, c: (i, k - 1, c)),
    )

    block = rows // 4
    w0, give = call(
        functools.partial(restrict_kernel, quarters, rows),
        [jax.ShapeDtypeStruct((rows, gvectors // 2), screened.dtype)] * 2,
        (sphere_sizes, screened[0]),
        in_specs=[SMEM, pl.BlockSpec((block, gvectors), lambda r: (r, 0))],
        out_specs=[pl.BlockSpec((block, gvectors // 2), lambda r: (r, 0))] * 2,
        grid=(rows // block,),
    )
    w1 = swap(give)
    c_par = {g: swap(c_own[g]) for g in range(3)}

    def first(g, counts, blocks):
        return call(
            functools.partial(first_kernel, g, owners, quarters, counts),
            jax.ShapeDtypeStruct((2, group_size * bands, rows), jnp.float32),
            (*blocks, w0, w1),
        )

    def last(groups, accs, far):
        shape = (
            quarters,
            len(groups) * group_size,
            cbands // quarters // 2,
            bands,
        )
        conduction = [x[g] for g in groups for x in (c_own, c_par)]
        return call(
            functools.partial(last_kernel, len(groups), quarters, half),
            [jax.ShapeDtypeStruct(shape, jnp.float32)] * 2,
            (*accs, *far, w0, w1, *conduction),
        )

    def exchange(keep, give):
        keep = keep + swap(give)
        parts = [send(keep[d], lambda i, k, c: (i, k + d, c)) for d in (1, 3, 2)]
        return keep[0] + parts[0] + parts[1] + parts[2]

    accs = [first(g, 1, (own[g], ahead[g], behind[g])) for g in (1, 2)]
    both = exchange(*last((1, 2), accs, far))
    results = [
        send(
            both[(g - 1) * group_size : g * group_size],
            lambda i, k, c: (i - shift[g], k, c),
        )
        for g in (1, 2)
    ]
    acc = first(0, 2, (*v0, *up, *down))
    results.insert(0, exchange(*last((0,), [acc], far0)))
    return jnp.concatenate(results, 0)


def solution(mesh):
    return jax.shard_map(
        shards,
        mesh=mesh,
        in_specs=(P("kr", None, "kc"), P("kr", None, "kc"), P("kr", "kc", None), P()),
        out_specs=P("kr", "kc", None),
        check_vma=False,
    )
```

```python
import functools

import jax
import jax.numpy as jnp
from jax import lax
from jax.experimental import pallas as pl
from jax.experimental.pallas import tpu as pltpu
from jax.sharding import PartitionSpec as P


prefactor = 0.015625
AXES = ("kr", "kc")
VMEM = pl.BlockSpec(memory_space=pltpu.VMEM)
SMEM = pl.BlockSpec(memory_space=pltpu.SMEM)
CONTRACT_LAST = (((1,), (1,)), ((), ()))


def moves(owners, quarters, target):
    pairs = []
    for i in range(owners):
        for k in range(quarters):
            for c in range(2):
                ti, tk, tc = target(i, k, c)
                pairs.append(
                    (
                        (i * quarters + k) * 2 + c,
                        ((ti % owners) * quarters + tk % quarters) * 2 + tc,
                    )
                )
    return pairs


def turn(group, q, owners):
    return 1 if group == 0 or q < owners // 2 else -1


def where_am_i():
    place = lax.axis_index("kc")
    return lax.axis_index("kr"), lax.div(place, 2), lax.rem(place, 2)


def heading(group, owner, owners):
    return jnp.int32(1) if group == 0 else jnp.where(owner < owners // 2, 1, -1)


def restrict_kernel(quarters, rows, spheres_ref, slab_ref, mine_ref, give_ref):
    owner, quarter, core = where_am_i()
    sphere = spheres_ref[owner]
    block = slab_ref.shape[0]
    first = (2 * quarter + core) * rows + pl.program_id(0) * block
    row = first + lax.broadcasted_iota(jnp.int32, (block, rows), 0)
    col = lax.broadcasted_iota(jnp.int32, (block, rows), 1)
    row_inside = row < sphere
    even = core == 0
    for j in range(quarters):
        kept = []
        for t in range(2):
            at = (2 * j + t) * rows
            keep = row_inside & (at + col < sphere)
            x = slab_ref[:, at : at + rows].astype(jnp.float32)
            kept.append(jnp.where(keep, x, 0.0))
        span = pl.ds(j * rows, rows)
        mine_ref[:, span] = jnp.where(even, kept[0], kept[1]).astype(mine_ref.dtype)
        give_ref[:, span] = jnp.where(even, kept[1], kept[0]).astype(give_ref.dtype)


def forward_kernel(owners, half, a1, b1, a2, b2, up_ref, down_ref):
    owner, _, _ = where_am_i()
    for n, (a, b) in enumerate(((a1, b1), (a2, b2))):
        ahead_up = heading(n + 1, owner, owners) > 0

        @pl.when(ahead_up)
        def _():
            up_ref[n * half : (n + 1) * half] = a[:half]
            down_ref[n * half : (n + 1) * half] = b[half:]

        @pl.when(jnp.logical_not(ahead_up))
        def _():
            up_ref[n * half : (n + 1) * half] = b[:half]
            down_ref[n * half : (n + 1) * half] = a[half:]


def flat(x):
    x = x[...]
    return x.reshape(x.shape[0] * x.shape[1], x.shape[2])


def first_kernel(group, owners, quarters, counts, *refs):
    blocks, (w0, w1, acc) = refs[:-3], refs[-3:]
    owner, quarter, _ = where_am_i()
    rows = acc.shape[2]
    sigma = heading(group, owner, owners)
    columns = (
        quarter,
        lax.rem(quarter - sigma + quarters, quarters),
        lax.rem(quarter + sigma + quarters, quarters),
    )
    for s, w in enumerate((w0, w1)):
        base, size = 0, acc.shape[1]
        for h in range(counts):
            total = None
            for n in range(3):
                pieces = blocks[n * counts : (n + 1) * counts]
                at = pl.multiple_of(columns[n] * rows, rows)
                y = lax.dot_general(
                    flat(pieces[h]),
                    w[:, pl.ds(at, rows)],
                    CONTRACT_LAST,
                    preferred_element_type=jnp.float32,
                )
                total = y if total is None else total + y
            acc[s, base : base + size // counts] = total
            base += size // counts


def last_kernel(groups, quarters, half, *refs):
    accs, refs = refs[:groups], refs[groups:]
    far, (w0, w1), refs = refs[:2], refs[2:4], refs[4:]
    conduction, (keep_ref, give_ref) = refs[:-2], refs[-2:]
    _, quarter, core = where_am_i()
    bands, rows = far[0].shape[1:]
    at = pl.multiple_of(lax.rem(quarter + 2, quarters) * rows, rows)
    even = core == 0
    for g in range(groups):
        for h, x in enumerate(far):
            base = h * half * bands
            both = []
            for s, w in enumerate((w0, w1)):
                y = accs[g][s, base : base + half * bands] + lax.dot_general(
                    x[g * half : (g + 1) * half].reshape(half * bands, rows),
                    w[:, pl.ds(at, rows)],
                    CONTRACT_LAST,
                    preferred_element_type=jnp.float32,
                )
                high = y.astype(jnp.bfloat16)
                low = (y - high.astype(jnp.float32)).astype(jnp.bfloat16)
                both.append((high, low))
            for n in range(half):
                p = h * half + n
                part = None
                for s in range(2):
                    c = conduction[2 * g + s]
                    span = slice(n * bands, (n + 1) * bands)
                    y = lax.dot_general(
                        c[p],
                        jnp.concatenate([both[s][0][span], both[s][1][span]], 0),
                        CONTRACT_LAST,
                        preferred_element_type=jnp.float32,
                    )
                    part = y if part is None else part + y
                part = (part[:, :bands] + part[:, bands:]) * prefactor
                part = part.reshape(quarters, 2, -1, bands)
                for j in range(quarters):
                    d = lax.rem(j - quarter + quarters, quarters)
                    q = g * 2 * half + p
                    keep_ref[d, q] = jnp.where(even, part[j, 0], part[j, 1])
                    give_ref[d, q] = jnp.where(even, part[j, 1], part[j, 0])


def merge_kernel(keep0, got0, keep, got, *out):
    size = keep0.shape[1]
    for d, ref in enumerate(out):
        ref[:size] = keep0[d] + got0[d]
        ref[size:] = keep[d] + got[d]


def total_kernel(a, b, c, d, *out):
    size = out[0].shape[0]
    for g, ref in enumerate(out):
        span = slice(g * size, (g + 1) * size)
        ref[...] = a[span] + b[span] + c[span] + d[span]


def shards(pair_conduction, pair_valence, screened, sphere_sizes):
    owners = lax.axis_size("kr")
    quarters = lax.axis_size("kc") // 2
    rows, gvectors = screened.shape[1:]
    group_size = pair_valence.shape[0] // 3
    bands = pair_valence.shape[1]
    cbands = pair_conduction.shape[1]
    half = group_size // 2
    shift = (0, -1, 1)
    params = pltpu.CompilerParams(vmem_limit_bytes=24 * 2**20)

    def send(x, target):
        return lax.ppermute(x, AXES, moves(owners, quarters, target))

    def swap(x):
        return send(x, lambda i, k, c: (i, k, 1 - c))

    def call(body, out_shape, operands, in_specs=None, out_specs=None, **kw):
        many = isinstance(out_shape, list)
        return pl.pallas_call(
            body,
            in_specs=in_specs or [VMEM] * len(operands),
            out_specs=out_specs or ([VMEM] * len(out_shape) if many else VMEM),
            out_shape=out_shape,
            compiler_params=params,
            **kw,
        )(*operands)

    v = [pair_valence[g * group_size : (g + 1) * group_size] for g in range(3)]
    cond = [pair_conduction[g * group_size : (g + 1) * group_size] for g in range(3)]

    own, ahead, behind = {}, {}, {}
    for g in (1, 2):
        own[g] = send(v[g], lambda i, k, c: (i + shift[g], k, c))
    for g in (1, 2):
        ahead[g] = send(
            v[g],
            lambda i, k, c: (
                i + shift[g],
                k + turn(g, (i + shift[g]) % owners, owners),
                c,
            ),
        )
    c_own = {0: cond[0]}
    for g in (1, 2):
        c_own[g] = send(cond[g], lambda i, k, c: (i + shift[g], k, c))
    for g in (1, 2):
        behind[g] = send(own[g], lambda i, k, c: (i, k - turn(g, i, owners), c))
    v0 = [v[0][:half], v[0][half:]]
    up, down = [None, None], [None, None]
    for n in range(2):
        up[n] = send(v0[n], lambda i, k, c: (i, k + 1, c))
        down[1 - n] = send(v0[1 - n], lambda i, k, c: (i, k - 1, c))
    going_up, going_down = call(
        functools.partial(forward_kernel, owners, half),
        [jax.ShapeDtypeStruct(v[0].shape, v[0].dtype)] * 2,
        (ahead[1], behind[1], ahead[2], behind[2]),
    )
    far = (
        send(going_up, lambda i, k, c: (i, k + 1, c)),
        send(going_down, lambda i, k, c: (i, k - 1, c)),
    )
    far0 = (
        send(up[0], lambda i, k, c: (i, k + 1, c)),
        send(down[1], lambda i, k, c: (i, k - 1, c)),
    )

    block = rows // 4
    w0, give = call(
        functools.partial(restrict_kernel, quarters, rows),
        [jax.ShapeDtypeStruct((rows, gvectors // 2), screened.dtype)] * 2,
        (sphere_sizes, screened[0]),
        in_specs=[SMEM, pl.BlockSpec((block, gvectors), lambda r: (r, 0))],
        out_specs=[pl.BlockSpec((block, gvectors // 2), lambda r: (r, 0))] * 2,
        grid=(rows // block,),
    )
    w1 = swap(give)
    c_par = {g: swap(c_own[g]) for g in range(3)}

    def first(g, counts, blocks):
        return call(
            functools.partial(first_kernel, g, owners, quarters, counts),
            jax.ShapeDtypeStruct((2, group_size * bands, rows), jnp.float32),
            (*blocks, w0, w1),
        )

    def last(groups, accs, far):
        shape = (
            quarters,
            len(groups) * group_size,
            cbands // quarters // 2,
            bands,
        )
        conduction = [x[g] for g in groups for x in (c_own, c_par)]
        return call(
            functools.partial(last_kernel, len(groups), quarters, half),
            [jax.ShapeDtypeStruct(shape, jnp.float32)] * 2,
            (*accs, *far, w0, w1, *conduction),
        )

    accs = [first(g, 1, (own[g], ahead[g], behind[g])) for g in (1, 2)]
    keep, give = last((1, 2), accs, far)
    got = swap(give)
    acc = first(0, 2, (*v0, *up, *down))
    keep0, give0 = last((0,), [acc], far0)
    got0 = swap(give0)
    block_shape = jax.ShapeDtypeStruct((3 * group_size, *keep.shape[2:]), jnp.float32)
    blocks = call(merge_kernel, [block_shape] * quarters, (keep0, got0, keep, got))
    others = [send(blocks[d], lambda i, k, c: (i, k + d, c)) for d in (1, 3, 2)]
    group_shape = jax.ShapeDtypeStruct((group_size, *keep.shape[2:]), jnp.float32)
    results = list(call(total_kernel, [group_shape] * 3, (blocks[0], *others)))
    for g in (1, 2):
        results[g] = send(results[g], lambda i, k, c: (i - shift[g], k, c))
    return jnp.concatenate(results, 0)


def solution(mesh):
    return jax.shard_map(
        shards,
        mesh=mesh,
        in_specs=(P("kr", None, "kc"), P("kr", None, "kc"), P("kr", "kc", None), P()),
        out_specs=P("kr", "kc", None),
        check_vma=False,
    )
```

```python
import functools

import jax
import jax.numpy as jnp
from jax import lax
from jax.experimental import pallas as pl
from jax.experimental.pallas import tpu as pltpu
from jax.sharding import PartitionSpec as P


prefactor = 0.015625
AXES = ("kr", "kc")
VMEM = pl.BlockSpec(memory_space=pltpu.VMEM)
SMEM = pl.BlockSpec(memory_space=pltpu.SMEM)
CONTRACT_LAST = (((1,), (1,)), ((), ()))


def moves(owners, quarters, target):
    pairs = []
    for i in range(owners):
        for k in range(quarters):
            for c in range(2):
                to = target(i, k, c)
                if to is None:
                    continue
                ti, tk, tc = to
                pairs.append(
                    (
                        (i * quarters + k) * 2 + c,
                        ((ti % owners) * quarters + tk % quarters) * 2 + tc,
                    )
                )
    return pairs


def turn(group, q, owners):
    return 1 if group == 0 or q < owners // 2 else -1


def crossing(owners):
    split = owners // 2
    low, high = (0, 1, split - 4, 4), (split - 1, split - 2, 3, split - 5)
    return {
        0: (1, owners - 1, low),
        split: (1, split - 1, tuple(split + m for m in low)),
        split - 1: (2, split, high),
        owners - 1: (2, 0, tuple(split + m for m in high)),
    }


def where_am_i():
    place = lax.axis_index("kc")
    return lax.axis_index("kr"), lax.div(place, 2), lax.rem(place, 2)


def heading(group, owner, owners):
    return jnp.int32(1) if group == 0 else jnp.where(owner < owners // 2, 1, -1)


def restrict_kernel(quarters, rows, spheres_ref, slab_ref, mine_ref, give_ref):
    owner, quarter, core = where_am_i()
    sphere = spheres_ref[owner]
    block = slab_ref.shape[0]
    first = (2 * quarter + core) * rows + pl.program_id(0) * block
    row = first + lax.broadcasted_iota(jnp.int32, (block, rows), 0)
    col = lax.broadcasted_iota(jnp.int32, (block, rows), 1)
    row_inside = row < sphere
    even = core == 0
    for j in range(quarters):
        kept = []
        for t in range(2):
            at = (2 * j + t) * rows
            keep = row_inside & (at + col < sphere)
            x = slab_ref[:, at : at + rows].astype(jnp.float32)
            kept.append(jnp.where(keep, x, 0.0))
        span = pl.ds(j * rows, rows)
        mine_ref[:, span] = jnp.where(even, kept[0], kept[1]).astype(mine_ref.dtype)
        give_ref[:, span] = jnp.where(even, kept[1], kept[0]).astype(give_ref.dtype)


def forward_kernel(owners, half, a1, b1, a2, b2, up_ref, down_ref):
    owner, _, _ = where_am_i()
    for n, (a, b) in enumerate(((a1, b1), (a2, b2))):
        ahead_up = heading(n + 1, owner, owners) > 0

        @pl.when(ahead_up)
        def _():
            up_ref[n * half : (n + 1) * half] = a[:half]
            down_ref[n * half : (n + 1) * half] = b[half:]

        @pl.when(jnp.logical_not(ahead_up))
        def _():
            up_ref[n * half : (n + 1) * half] = b[:half]
            down_ref[n * half : (n + 1) * half] = a[half:]


def pick_kernel(owners, c1, c2, *out):
    owner, _, _ = where_am_i()
    group1 = lax.rem(owner, owners // 2) == 0
    for c, flag in ((c1, group1), (c2, jnp.logical_not(group1))):

        @pl.when(flag)
        def _():
            for p, ref in enumerate(out):
                size = ref.shape[0]
                ref[...] = c[p * size : (p + 1) * size]


def place_kernel(owners, c1, c2, *refs):
    parts, out = refs[:-2], refs[-2:]
    owner, _, _ = where_am_i()
    split = owners // 2
    for c, ref, edge in ((c1, out[0], split - 1), (c2, out[1], 0)):
        crossed = lax.rem(owner, split) == edge

        @pl.when(crossed)
        def _():
            for p, part in enumerate(parts):
                size = part.shape[0]
                ref[p * size : (p + 1) * size] = part[...]

        @pl.when(jnp.logical_not(crossed))
        def _():
            ref[...] = c[...]


def flat(x):
    x = x[...]
    return x.reshape(x.shape[0] * x.shape[1], x.shape[2])


def first_kernel(group, owners, quarters, counts, *refs):
    blocks, (w0, w1, acc) = refs[:-3], refs[-3:]
    owner, quarter, _ = where_am_i()
    rows = acc.shape[2]
    sigma = heading(group, owner, owners)
    columns = (
        quarter,
        lax.rem(quarter - sigma + quarters, quarters),
        lax.rem(quarter + sigma + quarters, quarters),
    )
    for s, w in enumerate((w0, w1)):
        base, size = 0, acc.shape[1]
        for h in range(counts):
            total = None
            for n in range(3):
                pieces = blocks[n * counts : (n + 1) * counts]
                at = pl.multiple_of(columns[n] * rows, rows)
                y = lax.dot_general(
                    flat(pieces[h]),
                    w[:, pl.ds(at, rows)],
                    CONTRACT_LAST,
                    preferred_element_type=jnp.float32,
                )
                total = y if total is None else total + y
            acc[s, base : base + size // counts] = total
            base += size // counts


def last_kernel(groups, quarters, half, *refs):
    accs, refs = refs[:groups], refs[groups:]
    far, (w0, w1), refs = refs[:2], refs[2:4], refs[4:]
    conduction, (keep_ref, give_ref) = refs[:-2], refs[-2:]
    _, quarter, core = where_am_i()
    bands, rows = far[0].shape[1:]
    at = pl.multiple_of(lax.rem(quarter + 2, quarters) * rows, rows)
    even = core == 0
    for g in range(groups):
        for h, x in enumerate(far):
            base = h * half * bands
            both = []
            for s, w in enumerate((w0, w1)):
                y = accs[g][s, base : base + half * bands] + lax.dot_general(
                    x[g * half : (g + 1) * half].reshape(half * bands, rows),
                    w[:, pl.ds(at, rows)],
                    CONTRACT_LAST,
                    preferred_element_type=jnp.float32,
                )
                high = y.astype(jnp.bfloat16)
                low = (y - high.astype(jnp.float32)).astype(jnp.bfloat16)
                both.append((high, low))
            for n in range(half):
                p = h * half + n
                part = None
                for s in range(2):
                    c = conduction[2 * g + s]
                    span = slice(n * bands, (n + 1) * bands)
                    y = lax.dot_general(
                        c[p],
                        jnp.concatenate([both[s][0][span], both[s][1][span]], 0),
                        CONTRACT_LAST,
                        preferred_element_type=jnp.float32,
                    )
                    part = y if part is None else part + y
                part = (part[:, :bands] + part[:, bands:]) * prefactor
                part = part.reshape(quarters, 2, -1, bands)
                for j in range(quarters):
                    d = lax.rem(j - quarter + quarters, quarters)
                    q = g * 2 * half + p
                    keep_ref[d, q] = jnp.where(even, part[j, 0], part[j, 1])
                    give_ref[d, q] = jnp.where(even, part[j, 1], part[j, 0])


def merge_kernel(keep0, got0, keep, got, *out):
    size = keep0.shape[1]
    for d, ref in enumerate(out):
        ref[:size] = keep0[d] + got0[d]
        ref[size:] = keep[d] + got[d]


def total_kernel(a, b, c, d, *out):
    size = out[0].shape[0]
    for g, ref in enumerate(out):
        span = slice(g * size, (g + 1) * size)
        ref[...] = a[span] + b[span] + c[span] + d[span]


def shards(pair_conduction, pair_valence, screened, sphere_sizes):
    owners = lax.axis_size("kr")
    quarters = lax.axis_size("kc") // 2
    rows, gvectors = screened.shape[1:]
    group_size = pair_valence.shape[0] // 3
    bands = pair_valence.shape[1]
    cbands = pair_conduction.shape[1]
    half = group_size // 2
    shift = (0, -1, 1)
    params = pltpu.CompilerParams(vmem_limit_bytes=24 * 2**20)

    def send(x, target):
        return lax.ppermute(x, AXES, moves(owners, quarters, target))

    def swap(x):
        return send(x, lambda i, k, c: (i, k, 1 - c))

    def call(body, out_shape, operands, in_specs=None, out_specs=None, **kw):
        many = isinstance(out_shape, list)
        return pl.pallas_call(
            body,
            in_specs=in_specs or [VMEM] * len(operands),
            out_specs=out_specs or ([VMEM] * len(out_shape) if many else VMEM),
            out_shape=out_shape,
            compiler_params=params,
            **kw,
        )(*operands)

    v = [pair_valence[g * group_size : (g + 1) * group_size] for g in range(3)]
    cond = [pair_conduction[g * group_size : (g + 1) * group_size] for g in range(3)]

    own, ahead, behind = {}, {}, {}
    for g in (1, 2):
        own[g] = send(v[g], lambda i, k, c: (i + shift[g], k, c))
    for g in (1, 2):
        ahead[g] = send(
            v[g],
            lambda i, k, c: (
                i + shift[g],
                k + turn(g, (i + shift[g]) % owners, owners),
                c,
            ),
        )
    edges = crossing(owners)
    straight = {}
    for g in (1, 2):
        straight[g] = send(
            cond[g],
            lambda i, k, c: (
                None if i in edges and edges[i][0] == g else (i + shift[g], k, c)
            ),
        )
    count = len(edges[0][2])
    part = jax.ShapeDtypeStruct((group_size // count, *cond[0].shape[1:]), cond[0].dtype)
    parts = list(
        call(functools.partial(pick_kernel, owners), [part] * count, (cond[1], cond[2]))
    )
    for p in range(count):
        relays = {i: e[2][p] for i, e in edges.items()}
        if any(i != m for i, m in relays.items()):
            parts[p] = send(
                parts[p], lambda i, k, c: (relays[i], k, c) if i in relays else None
            )
        ends = {e[2][p]: e[1] for e in edges.values()}
        parts[p] = send(
            parts[p], lambda i, k, c: (ends[i], k, c) if i in ends else None
        )
    whole = jax.ShapeDtypeStruct(cond[0].shape, cond[0].dtype)
    c_own = {0: cond[0]}
    c_own[1], c_own[2] = call(
        functools.partial(place_kernel, owners),
        [whole] * 2,
        (straight[1], straight[2], *parts),
    )
    for g in (1, 2):
        behind[g] = send(own[g], lambda i, k, c: (i, k - turn(g, i, owners), c))
    v0 = [v[0][:half], v[0][half:]]
    up, down = [None, None], [None, None]
    for n in range(2):
        up[n] = send(v0[n], lambda i, k, c: (i, k + 1, c))
        down[1 - n] = send(v0[1 - n], lambda i, k, c: (i, k - 1, c))
    going_up, going_down = call(
        functools.partial(forward_kernel, owners, half),
        [jax.ShapeDtypeStruct(v[0].shape, v[0].dtype)] * 2,
        (ahead[1], behind[1], ahead[2], behind[2]),
    )
    far = (
        send(going_up, lambda i, k, c: (i, k + 1, c)),
        send(going_down, lambda i, k, c: (i, k - 1, c)),
    )
    far0 = (
        send(up[0], lambda i, k, c: (i, k + 1, c)),
        send(down[1], lambda i, k, c: (i, k - 1, c)),
    )

    block = rows // 4
    w0, give = call(
        functools.partial(restrict_kernel, quarters, rows),
        [jax.ShapeDtypeStruct((rows, gvectors // 2), screened.dtype)] * 2,
        (sphere_sizes, screened[0]),
        in_specs=[SMEM, pl.BlockSpec((block, gvectors), lambda r: (r, 0))],
        out_specs=[pl.BlockSpec((block, gvectors // 2), lambda r: (r, 0))] * 2,
        grid=(rows // block,),
    )
    w1 = swap(give)
    c_par = {g: swap(c_own[g]) for g in range(3)}

    def first(g, counts, blocks):
        return call(
            functools.partial(first_kernel, g, owners, quarters, counts),
            jax.ShapeDtypeStruct((2, group_size * bands, rows), jnp.float32),
            (*blocks, w0, w1),
        )

    def last(groups, accs, far):
        shape = (
            quarters,
            len(groups) * group_size,
            cbands // quarters // 2,
            bands,
        )
        conduction = [x[g] for g in groups for x in (c_own, c_par)]
        return call(
            functools.partial(last_kernel, len(groups), quarters, half),
            [jax.ShapeDtypeStruct(shape, jnp.float32)] * 2,
            (*accs, *far, w0, w1, *conduction),
        )

    accs = [first(g, 1, (own[g], ahead[g], behind[g])) for g in (1, 2)]
    keep, give = last((1, 2), accs, far)
    got = swap(give)
    acc = first(0, 2, (*v0, *up, *down))
    keep0, give0 = last((0,), [acc], far0)
    got0 = swap(give0)
    block_shape = jax.ShapeDtypeStruct((3 * group_size, *keep.shape[2:]), jnp.float32)
    blocks = call(merge_kernel, [block_shape] * quarters, (keep0, got0, keep, got))
    others = [send(blocks[d], lambda i, k, c: (i, k + d, c)) for d in (1, 3, 2)]
    group_shape = jax.ShapeDtypeStruct((group_size, *keep.shape[2:]), jnp.float32)
    results = list(call(total_kernel, [group_shape] * 3, (blocks[0], *others)))
    for g in (1, 2):
        results[g] = send(results[g], lambda i, k, c: (i - shift[g], k, c))
    return jnp.concatenate(results, 0)


def solution(mesh):
    return jax.shard_map(
        shards,
        mesh=mesh,
        in_specs=(P("kr", None, "kc"), P("kr", None, "kc"), P("kr", "kc", None), P()),
        out_specs=P("kr", "kc", None),
        check_vma=False,
    )
```

```python
import functools

import jax
import jax.numpy as jnp
from jax import lax
from jax.experimental import pallas as pl
from jax.experimental.pallas import tpu as pltpu
from jax.sharding import PartitionSpec as P


prefactor = 0.015625
AXES = ("kr", "kc")
VMEM = pl.BlockSpec(memory_space=pltpu.VMEM)
SMEM = pl.BlockSpec(memory_space=pltpu.SMEM)
CONTRACT_LAST = (((1,), (1,)), ((), ()))


def moves(owners, quarters, target):
    pairs = []
    for i in range(owners):
        for k in range(quarters):
            for c in range(2):
                to = target(i, k, c)
                if to is None:
                    continue
                ti, tk, tc = to
                pairs.append(
                    (
                        (i * quarters + k) * 2 + c,
                        ((ti % owners) * quarters + tk % quarters) * 2 + tc,
                    )
                )
    return pairs


def turn(group, q, owners):
    return 1 if group == 0 or q < owners // 2 else -1


def crossing(owners):
    split = owners // 2
    low, high = (0, 1, split - 4, 4), (split - 1, split - 2, 3, split - 5)
    return {
        0: (1, owners - 1, low),
        split: (1, split - 1, tuple(split + m for m in low)),
        split - 1: (2, split, high),
        owners - 1: (2, 0, tuple(split + m for m in high)),
    }


def where_am_i():
    place = lax.axis_index("kc")
    return lax.axis_index("kr"), lax.div(place, 2), lax.rem(place, 2)


def heading(group, owner, owners):
    return jnp.int32(1) if group == 0 else jnp.where(owner < owners // 2, 1, -1)


def restrict_kernel(quarters, rows, spheres_ref, slab_ref, mine_ref, give_ref):
    owner, quarter, core = where_am_i()
    sphere = spheres_ref[owner]
    block = slab_ref.shape[0]
    first = (2 * quarter + core) * rows + pl.program_id(0) * block
    row = first + lax.broadcasted_iota(jnp.int32, (block, rows), 0)
    col = lax.broadcasted_iota(jnp.int32, (block, rows), 1)
    row_inside = row < sphere
    even = core == 0
    for j in range(quarters):
        kept = []
        for t in range(2):
            at = (2 * j + t) * rows
            keep = row_inside & (at + col < sphere)
            x = slab_ref[:, at : at + rows].astype(jnp.float32)
            kept.append(jnp.where(keep, x, 0.0))
        span = pl.ds(j * rows, rows)
        mine_ref[:, span] = jnp.where(even, kept[0], kept[1]).astype(mine_ref.dtype)
        give_ref[:, span] = jnp.where(even, kept[1], kept[0]).astype(give_ref.dtype)


def forward_kernel(owners, half, a1, b1, a2, b2, up_ref, down_ref):
    owner, _, _ = where_am_i()
    for n, (a, b) in enumerate(((a1, b1), (a2, b2))):
        ahead_up = heading(n + 1, owner, owners) > 0

        @pl.when(ahead_up)
        def _():
            up_ref[n * half : (n + 1) * half] = a[:half]
            down_ref[n * half : (n + 1) * half] = b[half:]

        @pl.when(jnp.logical_not(ahead_up))
        def _():
            up_ref[n * half : (n + 1) * half] = b[:half]
            down_ref[n * half : (n + 1) * half] = a[half:]


def pick_kernel(owners, c1, c2, *out):
    owner, _, _ = where_am_i()
    group1 = lax.rem(owner, owners // 2) == 0
    for c, flag in ((c1, group1), (c2, jnp.logical_not(group1))):

        @pl.when(flag)
        def _():
            for p, ref in enumerate(out):
                size = ref.shape[0]
                ref[...] = c[p * size : (p + 1) * size]


def place_kernel(owners, c1, c2, *refs):
    parts, out = refs[:-2], refs[-2:]
    owner, _, _ = where_am_i()
    split = owners // 2
    for c, ref, edge in ((c1, out[0], split - 1), (c2, out[1], 0)):
        crossed = lax.rem(owner, split) == edge

        @pl.when(crossed)
        def _():
            for p, part in enumerate(parts):
                size = part.shape[0]
                ref[p * size : (p + 1) * size] = part[...]

        @pl.when(jnp.logical_not(crossed))
        def _():
            ref[...] = c[...]


def flat(x):
    x = x[...]
    return x.reshape(x.shape[0] * x.shape[1], x.shape[2])


def first_kernel(group, owners, quarters, own, ahead, behind, w0, w1, acc):
    owner, quarter, _ = where_am_i()
    rows = acc.shape[2]
    sigma = heading(group, owner, owners)
    blocks = (
        (own, quarter),
        (ahead, lax.rem(quarter - sigma + quarters, quarters)),
        (behind, lax.rem(quarter + sigma + quarters, quarters)),
    )
    for s, w in enumerate((w0, w1)):
        total = None
        for x, column in blocks:
            at = pl.multiple_of(column * rows, rows)
            y = lax.dot_general(
                flat(x),
                w[:, pl.ds(at, rows)],
                CONTRACT_LAST,
                preferred_element_type=jnp.float32,
            )
            total = y if total is None else total + y
        acc[s] = total


def last_kernel(groups, quarters, half, *refs):
    accs, refs = refs[:groups], refs[groups:]
    far, (w0, w1), refs = refs[:2], refs[2:4], refs[4:]
    conduction, (keep_ref, give_ref) = refs[:-2], refs[-2:]
    _, quarter, core = where_am_i()
    bands, rows = far[0].shape[1:]
    at = pl.multiple_of(lax.rem(quarter + 2, quarters) * rows, rows)
    even = core == 0
    for g in range(groups):
        for h, x in enumerate(far):
            base = h * half * bands
            both = []
            for s, w in enumerate((w0, w1)):
                y = accs[g][s, base : base + half * bands] + lax.dot_general(
                    x[g * half : (g + 1) * half].reshape(half * bands, rows),
                    w[:, pl.ds(at, rows)],
                    CONTRACT_LAST,
                    preferred_element_type=jnp.float32,
                )
                high = y.astype(jnp.bfloat16)
                low = (y - high.astype(jnp.float32)).astype(jnp.bfloat16)
                both.append((high, low))
            for n in range(half):
                p = h * half + n
                part = None
                for s in range(2):
                    c = conduction[2 * g + s]
                    span = slice(n * bands, (n + 1) * bands)
                    y = lax.dot_general(
                        c[p],
                        jnp.concatenate([both[s][0][span], both[s][1][span]], 0),
                        CONTRACT_LAST,
                        preferred_element_type=jnp.float32,
                    )
                    part = y if part is None else part + y
                part = (part[:, :bands] + part[:, bands:]) * prefactor
                part = part.reshape(quarters, 2, -1, bands)
                for j in range(quarters):
                    d = lax.rem(j - quarter + quarters, quarters)
                    m, lane = g * half + p // 2, (p % 2) * bands
                    span = slice(lane, lane + bands)
                    keep_ref[d, m, :, span] = jnp.where(even, part[j, 0], part[j, 1])
                    give_ref[d, m, :, span] = jnp.where(even, part[j, 1], part[j, 0])


def add_kernel(keep, got, *out):
    size = out[0].shape[1]
    for g, ref in enumerate(out):
        span = slice(g * size, (g + 1) * size)
        ref[...] = keep[:, span] + got[:, span]


def merge_kernel(keep0, got0, back1, back2, *out):
    size = keep0.shape[1]
    for d, ref in enumerate(out):
        ref[:size] = keep0[d] + got0[d]
        ref[size : 2 * size] = back1[d]
        ref[2 * size :] = back2[d]


def total_kernel(a, b, c, d, out):
    bands = out.shape[2]
    for m in range(a.shape[0]):
        x = a[m] + b[m] + c[m] + d[m]
        out[2 * m] = x[:, :bands]
        out[2 * m + 1] = x[:, bands:]


def shards(pair_conduction, pair_valence, screened, sphere_sizes):
    owners = lax.axis_size("kr")
    quarters = lax.axis_size("kc") // 2
    rows, gvectors = screened.shape[1:]
    group_size = pair_valence.shape[0] // 3
    bands = pair_valence.shape[1]
    cbands = pair_conduction.shape[1]
    half = group_size // 2
    shift = (0, -1, 1)
    params = pltpu.CompilerParams(vmem_limit_bytes=24 * 2**20)

    def send(x, target):
        return lax.ppermute(x, AXES, moves(owners, quarters, target))

    def swap(x):
        return send(x, lambda i, k, c: (i, k, 1 - c))

    def call(body, out_shape, operands, in_specs=None, out_specs=None, **kw):
        many = isinstance(out_shape, list)
        return pl.pallas_call(
            body,
            in_specs=in_specs or [VMEM] * len(operands),
            out_specs=out_specs or ([VMEM] * len(out_shape) if many else VMEM),
            out_shape=out_shape,
            compiler_params=params,
            **kw,
        )(*operands)

    v = [pair_valence[g * group_size : (g + 1) * group_size] for g in range(3)]
    cond = [pair_conduction[g * group_size : (g + 1) * group_size] for g in range(3)]

    own, ahead, behind = {}, {}, {}
    for g in (1, 2):
        own[g] = send(v[g], lambda i, k, c: (i + shift[g], k, c))
    for g in (1, 2):
        ahead[g] = send(
            v[g],
            lambda i, k, c: (
                i + shift[g],
                k + turn(g, (i + shift[g]) % owners, owners),
                c,
            ),
        )
    edges = crossing(owners)
    straight = {}
    for g in (1, 2):
        straight[g] = send(
            cond[g],
            lambda i, k, c: (
                None if i in edges and edges[i][0] == g else (i + shift[g], k, c)
            ),
        )
    count = len(edges[0][2])
    part = jax.ShapeDtypeStruct((group_size // count, *cond[0].shape[1:]), cond[0].dtype)
    parts = list(
        call(functools.partial(pick_kernel, owners), [part] * count, (cond[1], cond[2]))
    )
    for p in range(count):
        relays = {i: e[2][p] for i, e in edges.items()}
        if any(i != m for i, m in relays.items()):
            parts[p] = send(
                parts[p], lambda i, k, c: (relays[i], k, c) if i in relays else None
            )
        ends = {e[2][p]: e[1] for e in edges.values()}
        parts[p] = send(
            parts[p], lambda i, k, c: (ends[i], k, c) if i in ends else None
        )
    whole = jax.ShapeDtypeStruct(cond[0].shape, cond[0].dtype)
    c_own = {0: cond[0]}
    c_own[1], c_own[2] = call(
        functools.partial(place_kernel, owners),
        [whole] * 2,
        (straight[1], straight[2], *parts),
    )
    for g in (1, 2):
        behind[g] = send(own[g], lambda i, k, c: (i, k - turn(g, i, owners), c))
    own[0] = v[0]
    ahead[0] = send(v[0], lambda i, k, c: (i, k + 1, c))
    behind[0] = send(v[0], lambda i, k, c: (i, k - 1, c))
    going_up, going_down = call(
        functools.partial(forward_kernel, owners, half),
        [jax.ShapeDtypeStruct(v[0].shape, v[0].dtype)] * 2,
        (ahead[1], behind[1], ahead[2], behind[2]),
    )
    far = (
        send(going_up, lambda i, k, c: (i, k + 1, c)),
        send(going_down, lambda i, k, c: (i, k - 1, c)),
    )
    far0 = (
        send(ahead[0][:half], lambda i, k, c: (i, k + 1, c)),
        send(behind[0][half:], lambda i, k, c: (i, k - 1, c)),
    )

    block = rows // 4
    w0, give = call(
        functools.partial(restrict_kernel, quarters, rows),
        [jax.ShapeDtypeStruct((rows, gvectors // 2), screened.dtype)] * 2,
        (sphere_sizes, screened[0]),
        in_specs=[SMEM, pl.BlockSpec((block, gvectors), lambda r: (r, 0))],
        out_specs=[pl.BlockSpec((block, gvectors // 2), lambda r: (r, 0))] * 2,
        grid=(rows // block,),
    )
    w1 = swap(give)
    c_par = {g: swap(c_own[g]) for g in range(3)}

    def first(g):
        return call(
            functools.partial(first_kernel, g, owners, quarters),
            jax.ShapeDtypeStruct((2, group_size * bands, rows), jnp.float32),
            (own[g], ahead[g], behind[g], w0, w1),
        )

    def last(groups, accs, far):
        shape = (
            quarters,
            len(groups) * half,
            cbands // quarters // 2,
            2 * bands,
        )
        conduction = [x[g] for g in groups for x in (c_own, c_par)]
        return call(
            functools.partial(last_kernel, len(groups), quarters, half),
            [jax.ShapeDtypeStruct(shape, jnp.float32)] * 2,
            (*accs, *far, w0, w1, *conduction),
        )

    accs = [first(g) for g in (1, 2)]
    keep, give = last((1, 2), accs, far)
    packed = (quarters, half, *keep.shape[2:])
    back = list(
        call(
            add_kernel,
            [jax.ShapeDtypeStruct(packed, jnp.float32)] * 2,
            (keep, swap(give)),
        )
    )
    for g in (1, 2):
        back[g - 1] = send(back[g - 1], lambda i, k, c: (i - shift[g], k, c))
    acc = first(0)
    keep0, give0 = last((0,), [acc], far0)
    blocks = call(
        merge_kernel,
        [jax.ShapeDtypeStruct((3 * half, *packed[2:]), jnp.float32)] * quarters,
        (keep0, swap(give0), *back),
    )
    others = [send(blocks[d], lambda i, k, c: (i, k + d, c)) for d in (1, 3, 2)]
    return call(
        total_kernel,
        jax.ShapeDtypeStruct((3 * group_size, packed[2], bands), jnp.float32),
        (blocks[0], *others),
    )


def solution(mesh):
    return jax.shard_map(
        shards,
        mesh=mesh,
        in_specs=(P("kr", None, "kc"), P("kr", None, "kc"), P("kr", "kc", None), P()),
        out_specs=P("kr", "kc", None),
        check_vma=False,
    )
```

```python
import functools

import jax
import jax.numpy as jnp
from jax import lax
from jax.experimental import pallas as pl
from jax.experimental.pallas import tpu as pltpu
from jax.sharding import PartitionSpec as P


prefactor = 0.015625
AXES = ("kr", "kc")
VMEM = pl.BlockSpec(memory_space=pltpu.VMEM)
SMEM = pl.BlockSpec(memory_space=pltpu.SMEM)
CONTRACT_LAST = (((1,), (1,)), ((), ()))


def moves(owners, quarters, target):
    pairs = []
    for i in range(owners):
        for k in range(quarters):
            for c in range(2):
                to = target(i, k, c)
                if to is None:
                    continue
                ti, tk, tc = to
                pairs.append(
                    (
                        (i * quarters + k) * 2 + c,
                        ((ti % owners) * quarters + tk % quarters) * 2 + tc,
                    )
                )
    return pairs


def turn(group, q, owners):
    return 1 if group == 0 or q < owners // 2 else -1


def crossing(owners):
    split = owners // 2
    low, high = (0, 1, split - 4, 4), (split - 1, split - 2, 3, split - 5)
    return {
        0: (1, owners - 1, low),
        split: (1, split - 1, tuple(split + m for m in low)),
        split - 1: (2, split, high),
        owners - 1: (2, 0, tuple(split + m for m in high)),
    }


def where_am_i():
    place = lax.axis_index("kc")
    return lax.axis_index("kr"), lax.div(place, 2), lax.rem(place, 2)


def heading(group, owner, owners):
    return jnp.int32(1) if group == 0 else jnp.where(owner < owners // 2, 1, -1)


def restrict_kernel(quarters, rows, spheres_ref, slab_ref, mine_ref, give_ref):
    owner, quarter, core = where_am_i()
    sphere = spheres_ref[owner]
    block = slab_ref.shape[0]
    first = (2 * quarter + core) * rows + pl.program_id(0) * block
    row = first + lax.broadcasted_iota(jnp.int32, (block, rows), 0)
    col = lax.broadcasted_iota(jnp.int32, (block, rows), 1)
    row_inside = row < sphere
    even = core == 0
    for j in range(quarters):
        kept = []
        for t in range(2):
            at = (2 * j + t) * rows
            keep = row_inside & (at + col < sphere)
            x = slab_ref[:, at : at + rows].astype(jnp.float32)
            kept.append(jnp.where(keep, x, 0.0))
        span = pl.ds(j * rows, rows)
        mine_ref[:, span] = jnp.where(even, kept[0], kept[1]).astype(mine_ref.dtype)
        give_ref[:, span] = jnp.where(even, kept[1], kept[0]).astype(give_ref.dtype)


def forward_kernel(group, owners, a, b, up_ref, down_ref):
    owner, _, _ = where_am_i()
    half = up_ref.shape[0]
    ahead_up = heading(group, owner, owners) > 0

    @pl.when(ahead_up)
    def _():
        up_ref[...] = a[:half]
        down_ref[...] = b[half:]

    @pl.when(jnp.logical_not(ahead_up))
    def _():
        up_ref[...] = b[:half]
        down_ref[...] = a[half:]


def pick_kernel(owners, c1, c2, *out):
    owner, _, _ = where_am_i()
    group1 = lax.rem(owner, owners // 2) == 0
    for c, flag in ((c1, group1), (c2, jnp.logical_not(group1))):

        @pl.when(flag)
        def _():
            for p, ref in enumerate(out):
                size = ref.shape[0]
                ref[...] = c[p * size : (p + 1) * size]


def place_kernel(owners, c1, c2, *refs):
    parts, out = refs[:-2], refs[-2:]
    owner, _, _ = where_am_i()
    split = owners // 2
    for c, ref, edge in ((c1, out[0], split - 1), (c2, out[1], 0)):
        crossed = lax.rem(owner, split) == edge

        @pl.when(crossed)
        def _():
            for p, part in enumerate(parts):
                size = part.shape[0]
                ref[p * size : (p + 1) * size] = part[...]

        @pl.when(jnp.logical_not(crossed))
        def _():
            ref[...] = c[...]


def flat(x):
    x = x[...]
    return x.reshape(x.shape[0] * x.shape[1], x.shape[2])


def first_kernel(group, owners, quarters, own, ahead, behind, w0, w1, acc):
    owner, quarter, _ = where_am_i()
    rows = acc.shape[2]
    sigma = heading(group, owner, owners)
    blocks = (
        (own, quarter),
        (ahead, lax.rem(quarter - sigma + quarters, quarters)),
        (behind, lax.rem(quarter + sigma + quarters, quarters)),
    )
    for s, w in enumerate((w0, w1)):
        total = None
        for x, column in blocks:
            at = pl.multiple_of(column * rows, rows)
            y = lax.dot_general(
                flat(x),
                w[:, pl.ds(at, rows)],
                CONTRACT_LAST,
                preferred_element_type=jnp.float32,
            )
            total = y if total is None else total + y
        acc[s] = total


def last_kernel(groups, quarters, half, *refs):
    accs, refs = refs[:groups], refs[groups:]
    fars, refs = refs[: 2 * groups], refs[2 * groups :]
    (w0, w1), refs = refs[:2], refs[2:]
    conduction, (keep_ref, give_ref) = refs[:-2], refs[-2:]
    _, quarter, core = where_am_i()
    bands, rows = fars[0].shape[1:]
    at = pl.multiple_of(lax.rem(quarter + 2, quarters) * rows, rows)
    even = core == 0
    for g in range(groups):
        for h, x in enumerate(fars[2 * g : 2 * g + 2]):
            base = h * half * bands
            both = []
            for s, w in enumerate((w0, w1)):
                y = accs[g][s, base : base + half * bands] + lax.dot_general(
                    flat(x),
                    w[:, pl.ds(at, rows)],
                    CONTRACT_LAST,
                    preferred_element_type=jnp.float32,
                )
                high = y.astype(jnp.bfloat16)
                low = (y - high.astype(jnp.float32)).astype(jnp.bfloat16)
                both.append((high, low))
            for n in range(half):
                p = h * half + n
                part = None
                for s in range(2):
                    c = conduction[2 * g + s]
                    span = slice(n * bands, (n + 1) * bands)
                    y = lax.dot_general(
                        c[p],
                        jnp.concatenate([both[s][0][span], both[s][1][span]], 0),
                        CONTRACT_LAST,
                        preferred_element_type=jnp.float32,
                    )
                    part = y if part is None else part + y
                part = (part[:, :bands] + part[:, bands:]) * prefactor
                part = part.reshape(quarters, 2, -1, bands)
                for j in range(quarters):
                    d = lax.rem(j - quarter + quarters, quarters)
                    m, lane = g * half + p // 2, (p % 2) * bands
                    span = slice(lane, lane + bands)
                    keep_ref[d, m, :, span] = jnp.where(even, part[j, 0], part[j, 1])
                    give_ref[d, m, :, span] = jnp.where(even, part[j, 1], part[j, 0])


def add_kernel(keep, got, *out):
    size = out[0].shape[1]
    for g, ref in enumerate(out):
        span = slice(g * size, (g + 1) * size)
        ref[...] = keep[:, span] + got[:, span]


def merge_kernel(keep0, got0, back1, back2, *out):
    size = keep0.shape[1]
    for d, ref in enumerate(out):
        ref[:size] = keep0[d] + got0[d]
        ref[size : 2 * size] = back1[d]
        ref[2 * size :] = back2[d]


def total_kernel(a, b, c, d, out):
    bands = out.shape[2]
    for m in range(a.shape[0]):
        x = a[m] + b[m] + c[m] + d[m]
        out[2 * m] = x[:, :bands]
        out[2 * m + 1] = x[:, bands:]


def shards(pair_conduction, pair_valence, screened, sphere_sizes):
    owners = lax.axis_size("kr")
    quarters = lax.axis_size("kc") // 2
    rows, gvectors = screened.shape[1:]
    group_size = pair_valence.shape[0] // 3
    bands = pair_valence.shape[1]
    cbands = pair_conduction.shape[1]
    half = group_size // 2
    shift = (0, -1, 1)
    params = pltpu.CompilerParams(vmem_limit_bytes=24 * 2**20)

    def send(x, target):
        return lax.ppermute(x, AXES, moves(owners, quarters, target))

    def swap(x):
        return send(x, lambda i, k, c: (i, k, 1 - c))

    def call(body, out_shape, operands, in_specs=None, out_specs=None, **kw):
        many = isinstance(out_shape, list)
        return pl.pallas_call(
            body,
            in_specs=in_specs or [VMEM] * len(operands),
            out_specs=out_specs or ([VMEM] * len(out_shape) if many else VMEM),
            out_shape=out_shape,
            compiler_params=params,
            **kw,
        )(*operands)

    v = [pair_valence[g * group_size : (g + 1) * group_size] for g in range(3)]
    cond = [pair_conduction[g * group_size : (g + 1) * group_size] for g in range(3)]

    own, ahead, behind = {}, {}, {}
    for g in (1, 2):
        own[g] = send(v[g], lambda i, k, c: (i + shift[g], k, c))
    for g in (1, 2):
        ahead[g] = send(
            v[g],
            lambda i, k, c: (
                i + shift[g],
                k + turn(g, (i + shift[g]) % owners, owners),
                c,
            ),
        )
    edges = crossing(owners)
    straight = {}
    for g in (1, 2):
        straight[g] = send(
            cond[g],
            lambda i, k, c: (
                None if i in edges and edges[i][0] == g else (i + shift[g], k, c)
            ),
        )
    count = len(edges[0][2])
    part = jax.ShapeDtypeStruct((group_size // count, *cond[0].shape[1:]), cond[0].dtype)
    parts = list(
        call(functools.partial(pick_kernel, owners), [part] * count, (cond[1], cond[2]))
    )
    for p in range(count):
        relays = {i: e[2][p] for i, e in edges.items()}
        if any(i != m for i, m in relays.items()):
            parts[p] = send(
                parts[p], lambda i, k, c: (relays[i], k, c) if i in relays else None
            )
        ends = {e[2][p]: e[1] for e in edges.values()}
        parts[p] = send(
            parts[p], lambda i, k, c: (ends[i], k, c) if i in ends else None
        )
    whole = jax.ShapeDtypeStruct(cond[0].shape, cond[0].dtype)
    c_own = {0: cond[0]}
    c_own[1], c_own[2] = call(
        functools.partial(place_kernel, owners),
        [whole] * 2,
        (straight[1], straight[2], *parts),
    )
    for g in (1, 2):
        behind[g] = send(own[g], lambda i, k, c: (i, k - turn(g, i, owners), c))
    own[0] = v[0]
    ahead[0] = send(v[0], lambda i, k, c: (i, k + 1, c))
    behind[0] = send(v[0], lambda i, k, c: (i, k - 1, c))
    far = {}
    for g in (1, 2):
        going_up, going_down = call(
            functools.partial(forward_kernel, g, owners),
            [jax.ShapeDtypeStruct((half, *v[0].shape[1:]), v[0].dtype)] * 2,
            (ahead[g], behind[g]),
        )
        far[g] = (going_up, going_down)
    far[0] = (ahead[0][:half], behind[0][half:])
    for g in (1, 2, 0):
        far[g] = (
            send(far[g][0], lambda i, k, c: (i, k + 1, c)),
            send(far[g][1], lambda i, k, c: (i, k - 1, c)),
        )

    block = rows // 4
    w0, give = call(
        functools.partial(restrict_kernel, quarters, rows),
        [jax.ShapeDtypeStruct((rows, gvectors // 2), screened.dtype)] * 2,
        (sphere_sizes, screened[0]),
        in_specs=[SMEM, pl.BlockSpec((block, gvectors), lambda r: (r, 0))],
        out_specs=[pl.BlockSpec((block, gvectors // 2), lambda r: (r, 0))] * 2,
        grid=(rows // block,),
    )
    w1 = swap(give)
    c_par = {g: swap(c_own[g]) for g in range(3)}

    def first(g):
        return call(
            functools.partial(first_kernel, g, owners, quarters),
            jax.ShapeDtypeStruct((2, group_size * bands, rows), jnp.float32),
            (own[g], ahead[g], behind[g], w0, w1),
        )

    def last(groups, accs, far):
        shape = (
            quarters,
            len(groups) * half,
            cbands // quarters // 2,
            2 * bands,
        )
        conduction = [x[g] for g in groups for x in (c_own, c_par)]
        return call(
            functools.partial(last_kernel, len(groups), quarters, half),
            [jax.ShapeDtypeStruct(shape, jnp.float32)] * 2,
            (*accs, *far, w0, w1, *conduction),
        )

    accs = [first(g) for g in (1, 2)]
    keep, give = last((1, 2), accs, far[1] + far[2])
    packed = (quarters, half, *keep.shape[2:])
    back = list(
        call(
            add_kernel,
            [jax.ShapeDtypeStruct(packed, jnp.float32)] * 2,
            (keep, swap(give)),
        )
    )
    for g in (1, 2):
        back[g - 1] = send(back[g - 1], lambda i, k, c: (i - shift[g], k, c))
    acc = first(0)
    keep0, give0 = last((0,), [acc], far[0])
    blocks = call(
        merge_kernel,
        [jax.ShapeDtypeStruct((3 * half, *packed[2:]), jnp.float32)] * quarters,
        (keep0, swap(give0), *back),
    )
    others = [send(blocks[d], lambda i, k, c: (i, k + d, c)) for d in (1, 3, 2)]
    return call(
        total_kernel,
        jax.ShapeDtypeStruct((3 * group_size, packed[2], bands), jnp.float32),
        (blocks[0], *others),
    )


def solution(mesh):
    return jax.shard_map(
        shards,
        mesh=mesh,
        in_specs=(P("kr", None, "kc"), P("kr", None, "kc"), P("kr", "kc", None), P()),
        out_specs=P("kr", "kc", None),
        check_vma=False,
    )
```
